128 devices in a mesh: tm: 16 (over y, x), tile: 8 (over z, core).
Axes of the slice: x: 4, y: 4, z: 4, core: 2. Of those that a mesh axis runs over, the one named last changes fastest.
Arguments:
- queries: bfloat16 [16384, 1536], P(('tm', 'tile')), may hold values from -16 to 16
- keys: bfloat16 [16384, 1536], P(('tm', 'tile')), may hold values from -16 to 16
- values: bfloat16 [16384, 1536], P(('tm', 'tile')), may hold values from -6 to 6
- grad_out: bfloat16 [16384, 1536], P(('tm', 'tile')), may hold values from -6 to 6
- span_of_group: int32 [16], replicated, may hold values from 0 to 15, each once
- noise_level: int32 [16], replicated, may hold values from 0 to 999
- next_live: int32 [128], replicated, may hold values 0 or 1
- level_bias: float32 [1000, 12], replicated, may hold values from -2 to 2
Outputs:
- attended: bfloat16 [16384, 1536], P(('tm', 'tile'))
- grad_queries: bfloat16 [16384, 1536], P(('tm', 'tile'))
- grad_keys: bfloat16 [16384, 1536], P(('tm', 'tile'))
- grad_values: bfloat16 [16384, 1536], P(('tm', 'tile'))
The draws below stay inside these ranges and needn't reach their ends.
Inputs may be any that keep to these rules, and one draw needn't show every extreme that they name: span_of_group is a permutation of 0 to 15.
All inputs are finite; a program needn't handle non-finite values.
Results may differ from the reference program's by a relative error of at most 0.019.
Values may be sent and summed in bfloat16 or wider, within the bound.
A program may use at most 256 MiB of HBM per device.

```python
import math
import jax
import jax.numpy as jnp
from jax import lax

D = 1536
H = 12
HD = 128
LEVELS = 1000
TOK_DEV = 128
TOKENS = 16384
N_TM = 16
N_TILE = 8


def shared_fields(key):
    base_keys = jax.random.normal(jax.random.fold_in(key, 11), (TOKENS, D), jnp.float32)
    base_queries = jax.random.normal(jax.random.fold_in(key, 12), (TOKENS, D), jnp.float32)
    return (jnp.clip(base_queries, -6.0, 6.0), jnp.clip(base_keys, -6.0, 6.0))


def draw_queries(key, part):
    return shared_fields(key)[0].astype(jnp.bfloat16)


def draw_keys(key, part):
    return shared_fields(key)[1].astype(jnp.bfloat16)


def plant(result, key, low, top_value):
    spot = [jax.random.randint(jax.random.fold_in(key, axis), (), 0, length) for axis, length in enumerate(result.shape)]
    widest = result.shape.index(max(result.shape))
    beside = spot[:widest] + [(spot[widest] + 1) % result.shape[widest]] + spot[widest + 1:]
    return result.at[tuple(spot)].set(low).at[tuple(beside)].set(top_value)


def levels(key, extent, pieces, smallest, largest):
    def one(dim, shards_of):
        steps = jax.random.uniform(jax.random.fold_in(jax.random.fold_in(key, 6), dim), (shards_of,), jnp.float32, smallest / len(pieces), largest / len(pieces))
        return jnp.repeat(jnp.exp(steps), extent[dim] // shards_of).reshape((-1,) + (1,) * (len(extent) - dim - 1))

    factor_of = one(*pieces[0])
    for cut in pieces[1:]:
        factor_of = factor_of * one(*cut)
    return factor_of


def noise(stream_key, extent, deviation, reach, cuts=(), held_as=jnp.bfloat16):
    drawn = jax.random.normal(stream_key, extent, jnp.float32) * deviation
    if len(cuts) > 0:
        drawn = levels(stream_key, extent, cuts, -0.22, 0.18) * drawn
    return jnp.clip(drawn, min=-reach, max=reach).astype(held_as)


def setup_inputs(seed: int = 0) -> dict:
    streams_of = jax.random.split(jax.random.key(seed), 9)
    return {
        "queries": draw_queries(jax.random.fold_in(streams_of[8], 71), 0),
        "keys": draw_keys(jax.random.fold_in(streams_of[8], 71), 0),
        "values": noise(streams_of[2], (TOKENS, D), 1.0, 6.0, ((0, 128),)),
        "grad_out": noise(streams_of[3], (TOKENS, D), 1.0, 6.0, ((0, 128),)),
        "span_of_group": jax.random.permutation(streams_of[4], N_TM).astype(jnp.int32),
        "noise_level": plant(jax.random.randint(streams_of[5], (N_TM,), 0, LEVELS), jax.random.fold_in(streams_of[5], 1), 0, LEVELS - 1).astype(jnp.int32),
        "next_live": plant((jax.random.randint(streams_of[6], (N_TM * N_TILE,), 0, 2) < 1).astype(jnp.int32), jax.random.fold_in(streams_of[6], 1), 0, 1),
        "level_bias": jnp.clip(jax.random.uniform(streams_of[7], (LEVELS, H), jnp.float32, -2.0, 2.0), -2.0, 2.0),
    }


def reference(queries, keys, values, grad_out, span_of_group, noise_level, next_live, level_bias):
    inv_root = 1.0 / math.sqrt(HD)
    cube_shape = (N_TM, N_TILE, TOK_DEV, H, HD)
    query_cube = queries.reshape(cube_shape)
    key_cube = keys.reshape(cube_shape)
    value_cube = values.reshape(cube_shape)
    grad_cube = grad_out.reshape(cube_shape)
    near_keys = jnp.concatenate([key_cube, jnp.roll(key_cube, -1, axis=1)], axis=2)
    near_values = jnp.concatenate([value_cube, jnp.roll(value_cube, -1, axis=1)], axis=2)
    group_bias = level_bias[noise_level[span_of_group]]
    live_table = next_live.reshape(N_TM, N_TILE)
    second_half = jnp.arange(2 * TOK_DEV) >= TOK_DEV

    def one_tile(grad_carry, flat_index):
        key_grads, value_grads = grad_carry
        group_no = flat_index // N_TILE
        tile_no = flat_index % N_TILE
        q_rows = query_cube[group_no, tile_no].astype(jnp.float32)
        k_rows = near_keys[:, tile_no].astype(jnp.float32)
        v_rows = near_values[:, tile_no].astype(jnp.float32)
        g_rows = grad_cube[group_no, tile_no].astype(jnp.float32)
        attend = span_of_group <= span_of_group[group_no]
        key_mask = attend[:, None] & (jnp.logical_not(second_half)[None, :] | (live_table[group_no, tile_no] == 1))
        scores = jnp.einsum('qhe,jkhe->jhqk', q_rows, k_rows) * inv_root + group_bias[:, :, None, None]
        scores = jnp.where(key_mask[:, None, None, :], scores, -1e+30)
        row_peak = lax.optimization_barrier(jnp.max(scores, axis=(0, 3)))
        log_total = row_peak + jnp.log(lax.optimization_barrier(jnp.sum(jnp.exp(scores - row_peak[None, :, :, None]), axis=(0, 3))))
        weights_full = jnp.exp(scores - log_total[None, :, :, None])
        weights_low = lax.optimization_barrier(weights_full.astype(jnp.bfloat16)).astype(jnp.float32)
        attended = jnp.einsum('jhqk,jkhe->qhe', weights_low, v_rows).astype(jnp.bfloat16)
        row_delta = lax.optimization_barrier(jnp.sum(g_rows * attended.astype(jnp.float32), axis=2)).T
        grad_weights = jnp.einsum('qhe,jkhe->jhqk', g_rows, v_rows)
        grad_scores = (weights_full * (grad_weights - row_delta[None, :, :, None]) * inv_root).astype(jnp.bfloat16)
        grad_scores = lax.optimization_barrier(grad_scores).astype(jnp.float32)
        grad_query = jnp.einsum('jhqk,jkhe->qhe', grad_scores, k_rows).astype(jnp.bfloat16)
        key_part = jnp.einsum('jhqk,qhe->jkhe', grad_scores, q_rows)
        value_part = jnp.einsum('jhqk,qhe->jkhe', weights_low, g_rows)
        key_grads = key_grads.at[:, tile_no].add(key_part)
        value_grads = value_grads.at[:, tile_no].add(value_part)
        return ((key_grads, value_grads), (attended, grad_query))
    zero_grads = jnp.zeros((N_TM, N_TILE, 2 * TOK_DEV, H, HD), jnp.float32)
    (key_grads, value_grads), (attended, grad_query) = lax.scan(one_tile, (zero_grads, zero_grads), jnp.arange(N_TM * N_TILE, dtype=jnp.int32))
    key_total = key_grads[:, :, :TOK_DEV] + jnp.roll(key_grads[:, :, TOK_DEV:], 1, axis=1)
    value_total = value_grads[:, :, :TOK_DEV] + jnp.roll(value_grads[:, :, TOK_DEV:], 1, axis=1)
    return (attended.reshape(TOKENS, D), grad_query.reshape(TOKENS, D), key_total.astype(jnp.bfloat16).reshape(TOKENS, D), value_total.astype(jnp.bfloat16).reshape(TOKENS, D))
```

```python
import functools
import math

import jax
import jax.numpy as jnp
from jax import lax
from jax.experimental import pallas as pl
from jax.experimental.pallas import tpu as pltpu
from jax.sharding import PartitionSpec as P

SIDE = 4
GROUPS = 16
TILES = 8
HEADS = 12
ROWS = 128
WIDTH = 128
PAIR = 2 * ROWS
PAIRS = GROUPS // 2
NEG = -1e30
LOG2E = math.log2(math.e)
MESH = pl.DeviceIdType.MESH
OFFSETS = [(dy, dx) for dy in range(SIDE) for dx in range(SIDE) if (dy, dx) != (0, 0)]
ORDER = sorted(OFFSETS, key=lambda o: -(min(o[0], SIDE - o[0]) + min(o[1], SIDE - o[1])))


def head_of(y, x):
    skipped = SIDE - 1 - y
    return 3 * y + x - (x > skipped).astype(jnp.int32), x != skipped


def place():
    me = lax.axis_index("tm")
    tile = lax.axis_index("tile")
    return me, tile, lax.div(me, SIDE), lax.rem(me, SIDE)


def partner(y, x, dy, dx):
    py = lax.rem(y + dy, SIDE)
    px = lax.rem(x + dx, SIDE)
    head, live = head_of(py, px)
    return py * SIDE + px, head, live


def columns(head):
    return pl.ds(pl.multiple_of(head * WIDTH, WIDTH), WIDTH)


def meet(me, tile, y, x, before, after):
    barrier = pltpu.get_barrier_semaphore()
    for dy, dx in OFFSETS:
        other, _, _ = partner(y, x, dy, dx)
        pl.semaphore_signal(barrier, inc=1, device_id=(other, tile), device_id_type=MESH)
    for other in (before, after):
        pl.semaphore_signal(barrier, inc=1, device_id=(me, other), device_id_type=MESH)
    pl.semaphore_wait(barrier, len(OFFSETS) + 2)


def await_bytes(ref, sem):
    pltpu.make_async_copy(ref, ref, sem).wait()


def send(src, dst, send_sem, recv_sem, device):
    pltpu.make_async_remote_copy(
        src_ref=src, dst_ref=dst, send_sem=send_sem, recv_sem=recv_sem,
        device_id=device, device_id_type=MESH,
    ).start()


def spread_kernel(q_ref, k_ref, v_ref, g_ref, held, out_sem, kv_sem, qg_sem, near_out, near_in):
    me, tile, y, x = place()
    before = lax.rem(tile + TILES - 1, TILES)
    after = lax.rem(tile + 1, TILES)
    my_head, active = head_of(y, x)
    meet(me, tile, y, x, before, after)
    own = columns(my_head)

    @pl.when(active)
    def _():
        pltpu.make_async_copy(k_ref.at[:, own], held.at[2, me], kv_sem.at[me]).start()
        pltpu.make_async_copy(v_ref.at[:, own], held.at[3, me], kv_sem.at[me]).start()
        pltpu.make_async_copy(q_ref.at[:, own], held.at[0, me], qg_sem.at[me]).start()
        pltpu.make_async_copy(g_ref.at[:, own], held.at[1, me], qg_sem.at[me]).start()

    def give(pairs, recv_sem):
        for n, (dy, dx) in enumerate(ORDER):
            other, head, live = partner(y, x, dy, dx)

            @pl.when(live)
            def _(n=n, other=other, head=head):
                for ref, slot in pairs:
                    send(ref.at[:, columns(head)], held.at[slot, me], out_sem.at[n],
                         recv_sem.at[me], (other, tile))

    give([(k_ref, 2), (v_ref, 3)], kv_sem)
    give([(q_ref, 0), (g_ref, 1)], qg_sem)

    @pl.when(active)
    def _():
        sources = [partner(y, x, SIDE - dy, SIDE - dx)[0] for dy, dx in ORDER]
        for g in [me] + sources:
            await_bytes(held.at[pl.ds(2, 2), g], kv_sem.at[g])
            send(held.at[pl.ds(2, 2), g], held.at[pl.ds(4, 2), g], near_out.at[g],
                 near_in.at[g], (me, before))
        for g in [me] + sources:
            await_bytes(held.at[pl.ds(0, 2), g], qg_sem.at[g])
            await_bytes(held.at[pl.ds(2, 2), g], near_out.at[g])
            await_bytes(held.at[pl.ds(4, 2), g], near_in.at[g])

    for n, (dy, dx) in enumerate(ORDER):
        _, _, live = partner(y, x, dy, dx)

        @pl.when(live)
        def _(n=n):
            await_bytes(held.at[pl.ds(0, 4), 0], out_sem.at[n])


def spread(queries, keys, values, grad_out):
    dma = pltpu.SemaphoreType.DMA
    return pl.pallas_call(
        spread_kernel,
        out_shape=jax.ShapeDtypeStruct((6, GROUPS, ROWS, WIDTH), jnp.bfloat16),
        in_specs=[pl.BlockSpec(memory_space=pl.ANY)] * 4,
        out_specs=pl.BlockSpec(memory_space=pl.ANY),
        scratch_shapes=[dma((15,)), dma((GROUPS,)), dma((GROUPS,)), dma((GROUPS,)), dma((GROUPS,))],
        compiler_params=pltpu.CompilerParams(collective_id=0, has_side_effects=True),
        name="spread",
    )(queries, keys, values, grad_out)


def dot_nt(a, b):
    return lax.dot_general(a, b, (((1,), (1,)), ((), ())), preferred_element_type=jnp.float32)


def dot_nn(a, b):
    return lax.dot_general(a, b, (((1,), (0,)), ((), ())), preferred_element_type=jnp.float32)


def dot_tn(a, b):
    return lax.dot_general(a, b, (((0,), (0,)), ((), ())), preferred_element_type=jnp.float32)


def attend_kernel(span_ref, level_ref, live_ref, held, bias_ref, o_out, dq_out, own_out, near_out,
                  data, table, score, total, own_b, near_b, o_b, dq_b, order, in_sem, out_sem):
    me, tile, y, x = place()
    my_head, active = head_of(y, x)
    inv_root = 1.0 / math.sqrt(WIDTH)

    @pl.when(active)
    def _():
        for g in range(GROUPS):
            order[span_ref[g]] = g
        fetches = []
        for p in range(GROUPS):
            fetch = pltpu.make_async_copy(
                held.at[:, order[p]], data.at[:, pl.ds(p * ROWS, ROWS)], in_sem.at[p])
            fetch.start()
            fetches.append(fetch)
        lane = lax.broadcasted_iota(jnp.int32, (1, HEADS), 1)
        for p in range(GROUPS):
            row = bias_ref[pl.ds(level_ref[p], 1), :]
            value = jnp.sum(jnp.where(lane == my_head, row, 0.0), axis=1, keepdims=True) * LOG2E
            table[p // 2, :, pl.ds((p % 2) * ROWS, ROWS)] = jnp.broadcast_to(value, (8, ROWS))
        total[...] = jnp.zeros_like(total)
        for fetch in fetches:
            fetch.wait()

        upper = lax.broadcasted_iota(jnp.int32, (PAIR, 1), 0) < ROWS
        right = lax.broadcasted_iota(jnp.int32, (1, PAIR), 1) >= ROWS

        @pl.loop(0, PAIRS)
        def _(i):
            rows = pl.ds(pl.multiple_of(i * PAIR, PAIR), PAIR)
            q = data[0, rows, :]
            g = data[1, rows, :]
            live_a = live_ref[order[2 * i] * TILES + tile]
            live_b = live_ref[order[2 * i + 1] * TILES + tile]

            def half(near):
                sides = 2 if near else 1
                live_row = jnp.where(upper, live_a, live_b) == 1
                row_mask = jnp.where(live_row, 0.0, NEG)

                def scores(j, side, diagonal):
                    cols = pl.ds(pl.multiple_of(j * PAIR, PAIR), PAIR)
                    s = dot_nt(q, data[2 + 2 * side, cols, :]) * (inv_root * LOG2E)
                    s = s + table[j, 0:1, :]
                    if side:
                        s = s + row_mask
                    if diagonal:
                        s = jnp.where(jnp.logical_and(upper, right), NEG, s)
                    score[side, j] = s
                    return jnp.maximum(s[:, :ROWS], s[:, ROWS:])

                def pass_a(j, peak):
                    for side in range(sides):
                        peak = jnp.maximum(peak, scores(j, side, False))
                    return peak

                peak = scores(i, 0, True)
                if near:
                    peak = jnp.maximum(peak, scores(i, 1, True))
                peak = lax.fori_loop(0, i, pass_a, peak)
                row_peak = jnp.max(peak, axis=1, keepdims=True)

                def pass_b(j, carry):
                    denom, acc = carry
                    cols = pl.ds(pl.multiple_of(j * PAIR, PAIR), PAIR)
                    for side in range(sides):
                        e = jnp.exp2(score[side, j] - row_peak)
                        score[side, j] = e
                        denom = denom + (e[:, :ROWS] + e[:, ROWS:])
                        acc = acc + dot_nn(e.astype(jnp.bfloat16), data[3 + 2 * side, cols, :])
                    return denom, acc

                zero = jnp.zeros((PAIR, WIDTH), jnp.float32)
                denom, acc = lax.fori_loop(0, i + 1, pass_b, (zero, zero))
                recip = 1.0 / jnp.sum(denom, axis=1, keepdims=True)
                attended = (acc * recip).astype(jnp.bfloat16)
                o_b[rows, :] = attended
                delta = jnp.sum(g.astype(jnp.float32) * attended.astype(jnp.float32),
                                axis=1, keepdims=True)

                def pass_c(j, dq):
                    cols = pl.ds(pl.multiple_of(j * PAIR, PAIR), PAIR)
                    for side in range(sides):
                        dp = dot_nt(g, data[3 + 2 * side, cols, :])
                        w = score[side, j] * recip
                        ds = (w * (dp - delta)).astype(jnp.bfloat16)
                        dq = dq + dot_nn(ds, data[2 + 2 * side, cols, :])
                        total[2 * side, cols, :] += dot_tn(ds, q)
                        total[2 * side + 1, cols, :] += dot_tn(w.astype(jnp.bfloat16), g)
                    return dq

                dq = lax.fori_loop(0, i + 1, pass_c, zero)
                dq_b[rows, :] = (dq * inv_root).astype(jnp.bfloat16)

            any_live = (live_a + live_b) > 0
            pl.when(any_live)(lambda: half(True))
            pl.when(jnp.logical_not(any_live))(lambda: half(False))

        own_b[0] = total[0] * inv_root
        own_b[1] = total[1]
        near_b[0] = (total[2] * inv_root).astype(jnp.bfloat16)
        near_b[1] = total[3].astype(jnp.bfloat16)
        copies = []
        for p in range(GROUPS):
            here = pl.ds(p * ROWS, ROWS)
            for n, (src, dst) in enumerate([
                (near_b.at[:, here], near_out.at[:, order[p]]),
                (own_b.at[:, here], own_out.at[:, order[p]]),
                (o_b.at[here], o_out.at[order[p]]),
                (dq_b.at[here], dq_out.at[order[p]]),
            ]):
                copy = pltpu.make_async_copy(src, dst, out_sem.at[n, p])
                copy.start()
                copies.append(copy)
        for copy in copies:
            copy.wait()


def attend(span_of_group, noise_level, next_live, held, level_bias):
    smem = pl.BlockSpec(memory_space=pltpu.SMEM)
    hbm = pl.BlockSpec(memory_space=pl.ANY)
    tokens = GROUPS * ROWS
    dma = pltpu.SemaphoreType.DMA
    return pl.pallas_call(
        attend_kernel,
        out_shape=(
            jax.ShapeDtypeStruct((GROUPS, ROWS, WIDTH), jnp.bfloat16),
            jax.ShapeDtypeStruct((GROUPS, ROWS, WIDTH), jnp.bfloat16),
            jax.ShapeDtypeStruct((2, GROUPS, ROWS, WIDTH), jnp.float32),
            jax.ShapeDtypeStruct((2, GROUPS, ROWS, WIDTH), jnp.bfloat16),
        ),
        in_specs=[smem, smem, smem, hbm, pl.BlockSpec(memory_space=pltpu.VMEM)],
        out_specs=(hbm, hbm, hbm, hbm),
        scratch_shapes=[
            pltpu.VMEM((6, tokens, WIDTH), jnp.bfloat16),
            pltpu.VMEM((PAIRS, 8, PAIR), jnp.float32),
            pltpu.VMEM((2, PAIRS, PAIR, PAIR), jnp.float32),
            pltpu.VMEM((4, tokens, WIDTH), jnp.float32),
            pltpu.VMEM((2, tokens, WIDTH), jnp.float32),
            pltpu.VMEM((2, tokens, WIDTH), jnp.bfloat16),
            pltpu.VMEM((tokens, WIDTH), jnp.bfloat16),
            pltpu.VMEM((tokens, WIDTH), jnp.bfloat16),
            pltpu.SMEM((GROUPS,), jnp.int32),
            dma((GROUPS,)),
            dma((4, GROUPS)),
        ],
        compiler_params=pltpu.CompilerParams(vmem_limit_bytes=48 * 1024 * 1024),
        name="attend",
    )(span_of_group, noise_level, next_live, held, level_bias)


def collect_kernel(o_ref, dq_ref, own_ref, near_ref, o_out, dq_out, dk_out, dv_out,
                   landed, ready, near_out, near_in, out_a, out_b, in_a, in_b):
    me, tile, y, x = place()
    before = lax.rem(tile + TILES - 1, TILES)
    after = lax.rem(tile + 1, TILES)
    my_head, active = head_of(y, x)
    meet(me, tile, y, x, before, after)
    mine = columns(my_head)

    def line(dy):
        return pl.ds(pl.multiple_of(lax.rem(y + dy, SIDE) * SIDE, SIDE), SIDE)

    @pl.when(active)
    def _():
        for dy in (2, 1, 3, 0):
            send(near_ref.at[:, line(dy)], landed.at[:, line(dy)], near_out.at[dy],
                 near_in.at[dy], (me, after))
        for n, (dy, dx) in enumerate(ORDER):
            other, _, _ = partner(y, x, dy, dx)
            send(o_ref.at[other], o_out.at[:, mine], out_a.at[n], in_a.at[me], (other, tile))
            send(dq_ref.at[other], dq_out.at[:, mine], out_a.at[n], in_a.at[me], (other, tile))
        pltpu.make_async_copy(o_ref.at[me], o_out.at[:, mine], in_a.at[me]).start()
        pltpu.make_async_copy(dq_ref.at[me], dq_out.at[:, mine], in_a.at[me]).start()
        for dy in (2, 1, 3, 0):
            await_bytes(landed.at[:, line(dy)], near_in.at[dy])
            ready[:, line(dy)] = (
                own_ref[:, line(dy)] + landed[:, line(dy)].astype(jnp.float32)
            ).astype(jnp.bfloat16)
            for dx in (2, 1, 3, 0):
                if (dy, dx) == (0, 0):
                    pltpu.make_async_copy(ready.at[0, me], dk_out.at[:, mine], in_b.at[me]).start()
                    pltpu.make_async_copy(ready.at[1, me], dv_out.at[:, mine], in_b.at[me]).start()
                    continue
                n = ORDER.index((dy, dx))
                other, _, _ = partner(y, x, dy, dx)
                send(ready.at[0, other], dk_out.at[:, mine], out_b.at[n], in_b.at[me], (other, tile))
                send(ready.at[1, other], dv_out.at[:, mine], out_b.at[n], in_b.at[me], (other, tile))

    for chip in range(GROUPS):
        if chip % SIDE != SIDE - 1 - chip // SIDE:
            await_bytes(ready.at[:, 0], in_a.at[chip])
            await_bytes(ready.at[:, 0], in_b.at[chip])

    @pl.when(active)
    def _():
        for n in range(len(ORDER)):
            await_bytes(ready.at[:, 0], out_a.at[n])
            await_bytes(ready.at[:, 0], out_b.at[n])
        for dy in range(SIDE):
            await_bytes(landed.at[:, line(dy)], near_out.at[dy])


def collect(attended, grad_queries, own, near):
    hbm = pl.BlockSpec(memory_space=pl.ANY)
    dma = pltpu.SemaphoreType.DMA
    result = jax.ShapeDtypeStruct((ROWS, HEADS * WIDTH), jnp.bfloat16)
    return pl.pallas_call(
        collect_kernel,
        out_shape=(result,) * 4,
        in_specs=[hbm, hbm, pl.BlockSpec(memory_space=pltpu.VMEM), hbm],
        out_specs=(hbm,) * 4,
        scratch_shapes=[
            pltpu.VMEM((2, GROUPS, ROWS, WIDTH), jnp.bfloat16),
            pltpu.VMEM((2, GROUPS, ROWS, WIDTH), jnp.bfloat16),
            dma((SIDE,)), dma((SIDE,)), dma((15,)), dma((15,)), dma((GROUPS,)), dma((GROUPS,)),
        ],
        compiler_params=pltpu.CompilerParams(collective_id=1, has_side_effects=True),
        name="collect",
    )(attended, grad_queries, own, near)


def per_device(queries, keys, values, grad_out, span_of_group, noise_level, next_live, level_bias):
    held = spread(queries, keys, values, grad_out)
    attended, grad_queries, own, near = attend(span_of_group, noise_level, next_live, held, level_bias)
    return collect(attended, grad_queries, own, near)


def solution(mesh):
    rows = P(("tm", "tile"), None)
    return jax.shard_map(
        per_device, mesh=mesh,
        in_specs=(rows, rows, rows, rows, P(), P(), P(), P()),
        out_specs=(rows, rows, rows, rows), check_vma=False,
    )
```

```python
import functools
import math

import jax
import jax.numpy as jnp
from jax import lax
from jax.experimental import pallas as pl
from jax.experimental.pallas import tpu as pltpu
from jax.sharding import PartitionSpec as P

SIDE = 4
GROUPS = 16
TILES = 8
HEADS = 12
ROWS = 128
WIDTH = 128
PAIR = 2 * ROWS
PAIRS = GROUPS // 2
NEG = -1e30
LOG2E = math.log2(math.e)
MESH = pl.DeviceIdType.MESH
OFFSETS = [(dy, dx) for dy in range(SIDE) for dx in range(SIDE) if (dy, dx) != (0, 0)]
ORDER = sorted(OFFSETS, key=lambda o: -(min(o[0], SIDE - o[0]) + min(o[1], SIDE - o[1])))


def head_of(y, x):
    skipped = SIDE - 1 - y
    return 3 * y + x - (x > skipped).astype(jnp.int32), x != skipped


def place():
    me = lax.axis_index("tm")
    tile = lax.axis_index("tile")
    return me, tile, lax.div(me, SIDE), lax.rem(me, SIDE)


def partner(y, x, dy, dx):
    py = lax.rem(y + dy, SIDE)
    px = lax.rem(x + dx, SIDE)
    head, live = head_of(py, px)
    return py * SIDE + px, head, live


def columns(head):
    return pl.ds(pl.multiple_of(head * WIDTH, WIDTH), WIDTH)


def meet(me, tile, y, x, before, after):
    barrier = pltpu.get_barrier_semaphore()
    for dy, dx in OFFSETS:
        other, _, _ = partner(y, x, dy, dx)
        pl.semaphore_signal(barrier, inc=1, device_id=(other, tile), device_id_type=MESH)
    for other in (before, after):
        pl.semaphore_signal(barrier, inc=1, device_id=(me, other), device_id_type=MESH)
    pl.semaphore_wait(barrier, len(OFFSETS) + 2)


def await_bytes(ref, sem):
    pltpu.make_async_copy(ref, ref, sem).wait()


def send(src, dst, send_sem, recv_sem, device):
    pltpu.make_async_remote_copy(
        src_ref=src, dst_ref=dst, send_sem=send_sem, recv_sem=recv_sem,
        device_id=device, device_id_type=MESH,
    ).start()


def spread_kernel(q_ref, k_ref, v_ref, g_ref, held, out_sem, kv_sem, qg_sem, near_out, near_in):
    me, tile, y, x = place()
    before = lax.rem(tile + TILES - 1, TILES)
    after = lax.rem(tile + 1, TILES)
    my_head, active = head_of(y, x)
    meet(me, tile, y, x, before, after)
    own = columns(my_head)

    @pl.when(active)
    def _():
        pltpu.make_async_copy(k_ref.at[:, own], held.at[2, me], kv_sem.at[me]).start()
        pltpu.make_async_copy(v_ref.at[:, own], held.at[3, me], kv_sem.at[me]).start()
        pltpu.make_async_copy(q_ref.at[:, own], held.at[0, me], qg_sem.at[me]).start()
        pltpu.make_async_copy(g_ref.at[:, own], held.at[1, me], qg_sem.at[me]).start()

    def give(pairs, recv_sem):
        for n, (dy, dx) in enumerate(ORDER):
            other, head, live = partner(y, x, dy, dx)

            @pl.when(live)
            def _(n=n, other=other, head=head):
                for ref, slot in pairs:
                    send(ref.at[:, columns(head)], held.at[slot, me], out_sem.at[n],
                         recv_sem.at[me], (other, tile))

    give([(k_ref, 2), (v_ref, 3)], kv_sem)
    give([(q_ref, 0), (g_ref, 1)], qg_sem)

    @pl.when(active)
    def _():
        sources = [partner(y, x, SIDE - dy, SIDE - dx)[0] for dy, dx in ORDER]
        for g in [me] + sources:
            await_bytes(held.at[pl.ds(2, 2), g], kv_sem.at[g])
            send(held.at[pl.ds(2, 2), g], held.at[pl.ds(4, 2), g], near_out.at[g],
                 near_in.at[g], (me, before))
        for g in [me] + sources:
            await_bytes(held.at[pl.ds(0, 2), g], qg_sem.at[g])
            await_bytes(held.at[pl.ds(2, 2), g], near_out.at[g])
            await_bytes(held.at[pl.ds(4, 2), g], near_in.at[g])

    for n, (dy, dx) in enumerate(ORDER):
        _, _, live = partner(y, x, dy, dx)

        @pl.when(live)
        def _(n=n):
            await_bytes(held.at[pl.ds(0, 4), 0], out_sem.at[n])


def spread(queries, keys, values, grad_out):
    dma = pltpu.SemaphoreType.DMA
    return pl.pallas_call(
        spread_kernel,
        out_shape=jax.ShapeDtypeStruct((6, GROUPS, ROWS, WIDTH), jnp.bfloat16),
        in_specs=[pl.BlockSpec(memory_space=pl.ANY)] * 4,
        out_specs=pl.BlockSpec(memory_space=pl.ANY),
        scratch_shapes=[dma((15,)), dma((GROUPS,)), dma((GROUPS,)), dma((GROUPS,)), dma((GROUPS,))],
        compiler_params=pltpu.CompilerParams(collective_id=0, has_side_effects=True),
        name="spread",
    )(queries, keys, values, grad_out)


def dot_nt(a, b):
    return lax.dot_general(a, b, (((1,), (1,)), ((), ())), preferred_element_type=jnp.float32)


def dot_nn(a, b):
    return lax.dot_general(a, b, (((1,), (0,)), ((), ())), preferred_element_type=jnp.float32)


def attend_kernel(span_ref, level_ref, live_ref, held, bias_ref, o_out, dq_out, own_out, near_out,
                  data, flat, table, score, total, near_b, o_b, dq_b, order, in_sem, out_sem):
    me, tile, y, x = place()
    my_head, active = head_of(y, x)
    inv_root = 1.0 / math.sqrt(WIDTH)

    @pl.when(active)
    def _():
        for g in range(GROUPS):
            order[span_ref[g]] = g
        fetches = []
        for p in range(GROUPS):
            fetch = pltpu.make_async_copy(
                held.at[:, order[p]], data.at[:, pl.ds(p * ROWS, ROWS)], in_sem.at[p])
            fetch.start()
            fetches.append(fetch)
        lane = lax.broadcasted_iota(jnp.int32, (1, HEADS), 1)
        for p in range(GROUPS):
            row = bias_ref[pl.ds(level_ref[p], 1), :]
            value = jnp.sum(jnp.where(lane == my_head, row, 0.0), axis=1, keepdims=True) * LOG2E
            table[p] = jnp.broadcast_to(value, (8, ROWS))
        total[...] = jnp.zeros_like(total)
        for fetch in fetches:
            fetch.wait()

        @pl.loop(0, PAIRS)
        def _(j):
            cols = pl.ds(pl.multiple_of(j * PAIR, PAIR), PAIR)
            for n in range(4):
                flat[n, j] = data[2 + n, cols, :].T

        right = lax.broadcasted_iota(jnp.int32, (1, PAIR), 1) >= ROWS

        @pl.loop(0, PAIRS)
        def _(i):
            rows = pl.ds(pl.multiple_of(i * PAIR, PAIR), PAIR)
            q = data[0, rows, :]
            g = data[1, rows, :]
            live_a = live_ref[order[2 * i] * TILES + tile]
            live_b = live_ref[order[2 * i + 1] * TILES + tile]

            def half(near):
                sides = 2 if near else 1
                near_mask = jnp.where(jnp.where(right, live_b, live_a) == 1, 0.0, NEG)
                late_mask = jnp.where(right, 0.0, NEG)

                def scores(j, side, diagonal):
                    cols = pl.ds(pl.multiple_of(j * PAIR, PAIR), PAIR)
                    s = dot_nt(data[2 + 2 * side, cols, :], q) * (inv_root * LOG2E)
                    peak = None
                    for part in range(2):
                        bias = table[2 * j + part, 0:1, :]
                        bias = jnp.concatenate([bias, bias], axis=1)
                        if side:
                            bias = bias + near_mask
                        if diagonal and part:
                            bias = bias + late_mask
                        piece = s[part * ROWS:(part + 1) * ROWS] + bias
                        score[side, j, pl.ds(part * ROWS, ROWS), :] = piece
                        top = jnp.max(piece.reshape(ROWS // 8, 8, PAIR), axis=0)
                        peak = top if peak is None else jnp.maximum(peak, top)
                    return peak

                def pass_a(j, peak):
                    for side in range(sides):
                        peak = jnp.maximum(peak, scores(j, side, False))
                    return peak

                peak = scores(i, 0, True)
                if near:
                    peak = jnp.maximum(peak, scores(i, 1, True))
                peak = lax.fori_loop(0, i, pass_a, peak)
                peak = jnp.max(peak, axis=0, keepdims=True)

                def pass_b(j, carry):
                    denom, acc = carry
                    for side in range(sides):
                        e = jnp.exp2(score[side, j] - peak)
                        score[side, j] = e
                        denom = denom + jnp.sum(e.reshape(PAIR // 8, 8, PAIR), axis=0)
                        acc = acc + dot_nn(flat[2 * side + 1, j], e.astype(jnp.bfloat16))
                    return denom, acc

                zero = jnp.zeros((WIDTH, PAIR), jnp.float32)
                denom, acc = lax.fori_loop(
                    0, i + 1, pass_b, (jnp.zeros((8, PAIR), jnp.float32), zero))
                recip = 1.0 / jnp.sum(denom, axis=0, keepdims=True)
                attended = (acc * recip).astype(jnp.bfloat16)
                o_b[rows, :] = attended.T
                delta = jnp.sum(g.T.astype(jnp.float32) * attended.astype(jnp.float32),
                                axis=0, keepdims=True)

                def pass_c(j, dq):
                    cols = pl.ds(pl.multiple_of(j * PAIR, PAIR), PAIR)
                    for side in range(sides):
                        dp = dot_nt(data[3 + 2 * side, cols, :], g)
                        w = score[side, j] * recip
                        ds = (w * (dp - delta)).astype(jnp.bfloat16)
                        dq = dq + dot_nn(flat[2 * side, j], ds)
                        total[2 * side, cols, :] += dot_nn(ds, q)
                        total[2 * side + 1, cols, :] += dot_nn(w.astype(jnp.bfloat16), g)
                    return dq

                dq = lax.fori_loop(0, i + 1, pass_c, zero)
                dq_b[rows, :] = (dq * inv_root).astype(jnp.bfloat16).T

            any_live = (live_a + live_b) > 0
            pl.when(any_live)(lambda: half(True))
            pl.when(jnp.logical_not(any_live))(lambda: half(False))

        total[0] = total[0] * inv_root
        near_b[0] = (total[2] * inv_root).astype(jnp.bfloat16)
        near_b[1] = total[3].astype(jnp.bfloat16)
        copies = []
        for p in range(GROUPS):
            here = pl.ds(p * ROWS, ROWS)
            for n, (src, dst) in enumerate([
                (near_b.at[:, here], near_out.at[:, order[p]]),
                (total.at[pl.ds(0, 2), here], own_out.at[:, order[p]]),
                (o_b.at[here], o_out.at[order[p]]),
                (dq_b.at[here], dq_out.at[order[p]]),
            ]):
                copy = pltpu.make_async_copy(src, dst, out_sem.at[n, p])
                copy.start()
                copies.append(copy)
        for copy in copies:
            copy.wait()


def attend(span_of_group, noise_level, next_live, held, level_bias):
    smem = pl.BlockSpec(memory_space=pltpu.SMEM)
    hbm = pl.BlockSpec(memory_space=pl.ANY)
    tokens = GROUPS * ROWS
    dma = pltpu.SemaphoreType.DMA
    return pl.pallas_call(
        attend_kernel,
        out_shape=(
            jax.ShapeDtypeStruct((GROUPS, ROWS, WIDTH), jnp.bfloat16),
            jax.ShapeDtypeStruct((GROUPS, ROWS, WIDTH), jnp.bfloat16),
            jax.ShapeDtypeStruct((2, GROUPS, ROWS, WIDTH), jnp.float32),
            jax.ShapeDtypeStruct((2, GROUPS, ROWS, WIDTH), jnp.bfloat16),
        ),
        in_specs=[smem, smem, smem, hbm, pl.BlockSpec(memory_space=pltpu.VMEM)],
        out_specs=(hbm, hbm, hbm, hbm),
        scratch_shapes=[
            pltpu.VMEM((6, tokens, WIDTH), jnp.bfloat16),
            pltpu.VMEM((4, PAIRS, WIDTH, PAIR), jnp.bfloat16),
            pltpu.VMEM((GROUPS, 8, ROWS), jnp.float32),
            pltpu.VMEM((2, PAIRS, PAIR, PAIR), jnp.float32),
            pltpu.VMEM((4, tokens, WIDTH), jnp.float32),
            pltpu.VMEM((2, tokens, WIDTH), jnp.bfloat16),
            pltpu.VMEM((tokens, WIDTH), jnp.bfloat16),
            pltpu.VMEM((tokens, WIDTH), jnp.bfloat16),
            pltpu.SMEM((GROUPS,), jnp.int32),
            dma((GROUPS,)),
            dma((4, GROUPS)),
        ],
        compiler_params=pltpu.CompilerParams(vmem_limit_bytes=60 * 1024 * 1024),
        name="attend",
    )(span_of_group, noise_level, next_live, held, level_bias)


def collect_kernel(o_ref, dq_ref, own_ref, near_ref, o_out, dq_out, dk_out, dv_out,
                   landed, ready, near_out, near_in, out_a, out_b, in_a, in_b):
    me, tile, y, x = place()
    before = lax.rem(tile + TILES - 1, TILES)
    after = lax.rem(tile + 1, TILES)
    my_head, active = head_of(y, x)
    meet(me, tile, y, x, before, after)
    mine = columns(my_head)

    def line(dy):
        return pl.ds(pl.multiple_of(lax.rem(y + dy, SIDE) * SIDE, SIDE), SIDE)

    @pl.when(active)
    def _():
        for dy in (2, 1, 3, 0):
            send(near_ref.at[:, line(dy)], landed.at[:, line(dy)], near_out.at[dy],
                 near_in.at[dy], (me, after))
        for n, (dy, dx) in enumerate(ORDER):
            other, _, _ = partner(y, x, dy, dx)
            send(o_ref.at[other], o_out.at[:, mine], out_a.at[n], in_a.at[me], (other, tile))
            send(dq_ref.at[other], dq_out.at[:, mine], out_a.at[n], in_a.at[me], (other, tile))
        pltpu.make_async_copy(o_ref.at[me], o_out.at[:, mine], in_a.at[me]).start()
        pltpu.make_async_copy(dq_ref.at[me], dq_out.at[:, mine], in_a.at[me]).start()
        for dy in (2, 1, 3, 0):
            await_bytes(landed.at[:, line(dy)], near_in.at[dy])
            ready[:, line(dy)] = (
                own_ref[:, line(dy)] + landed[:, line(dy)].astype(jnp.float32)
            ).astype(jnp.bfloat16)
            for dx in (2, 1, 3, 0):
                if (dy, dx) == (0, 0):
                    pltpu.make_async_copy(ready.at[0, me], dk_out.at[:, mine], in_b.at[me]).start()
                    pltpu.make_async_copy(ready.at[1, me], dv_out.at[:, mine], in_b.at[me]).start()
                    continue
                n = ORDER.index((dy, dx))
                other, _, _ = partner(y, x, dy, dx)
                send(ready.at[0, other], dk_out.at[:, mine], out_b.at[n], in_b.at[me], (other, tile))
                send(ready.at[1, other], dv_out.at[:, mine], out_b.at[n], in_b.at[me], (other, tile))

    for chip in range(GROUPS):
        if chip % SIDE != SIDE - 1 - chip // SIDE:
            await_bytes(ready.at[:, 0], in_a.at[chip])
            await_bytes(ready.at[:, 0], in_b.at[chip])

    @pl.when(active)
    def _():
        for n in range(len(ORDER)):
            await_bytes(ready.at[:, 0], out_a.at[n])
            await_bytes(ready.at[:, 0], out_b.at[n])
        for dy in range(SIDE):
            await_bytes(landed.at[:, line(dy)], near_out.at[dy])


def collect(attended, grad_queries, own, near):
    hbm = pl.BlockSpec(memory_space=pl.ANY)
    dma = pltpu.SemaphoreType.DMA
    result = jax.ShapeDtypeStruct((ROWS, HEADS * WIDTH), jnp.bfloat16)
    return pl.pallas_call(
        collect_kernel,
        out_shape=(result,) * 4,
        in_specs=[hbm, hbm, pl.BlockSpec(memory_space=pltpu.VMEM), hbm],
        out_specs=(hbm,) * 4,
        scratch_shapes=[
            pltpu.VMEM((2, GROUPS, ROWS, WIDTH), jnp.bfloat16),
            pltpu.VMEM((2, GROUPS, ROWS, WIDTH), jnp.bfloat16),
            dma((SIDE,)), dma((SIDE,)), dma((15,)), dma((15,)), dma((GROUPS,)), dma((GROUPS,)),
        ],
        compiler_params=pltpu.CompilerParams(collective_id=1, has_side_effects=True),
        name="collect",
    )(attended, grad_queries, own, near)


def settle_kernel(*refs):
    for src, dst in zip(refs[:4], refs[4:]):
        dst[...] = src[...]


def settle(arrays):
    chunk = pl.BlockSpec((ROWS // 2, HEADS * WIDTH), lambda n: (n, 0))
    result = jax.ShapeDtypeStruct((ROWS, HEADS * WIDTH), jnp.bfloat16)
    return pl.pallas_call(
        settle_kernel, grid=(2,), out_shape=(result,) * 4,
        in_specs=[chunk] * 4, out_specs=(chunk,) * 4, name="settle",
    )(*arrays)


def per_device(queries, keys, values, grad_out, span_of_group, noise_level, next_live, level_bias):
    held = spread(queries, keys, values, grad_out)
    attended, grad_queries, own, near = attend(span_of_group, noise_level, next_live, held, level_bias)
    return settle(collect(attended, grad_queries, own, near))


def solution(mesh):
    rows = P(("tm", "tile"), None)
    return jax.shard_map(
        per_device, mesh=mesh,
        in_specs=(rows, rows, rows, rows, P(), P(), P(), P()),
        out_specs=(rows, rows, rows, rows), check_vma=False,
    )
```
